32 devices in a mesh: parts: 2 (over y), leaf: 16 (over z, x, core).
Axes of the slice: x: 2, y: 2, z: 4, core: 2. Of those that a mesh axis runs over, the one named last changes fastest.
Arguments:
- features: bfloat16 [32768, 512], P('leaf', 'parts'), parts along dimension 1, may hold values from -6 to 6
- vertex_order: int32 [16, 2048], P('leaf'), may hold values from 0 to 2047, each once within a row
- leaf_adjacency: int32 [16, 8, 3], P('leaf'), may hold values from 0 to 7
- near_blocks: bfloat16 [16, 8, 3, 256, 256], P('leaf'), may hold values from -0.21875 to 0.21875
- basis: bfloat16 [4, 32768, 256], P(None, 'leaf'), may hold values from -0.07432544 to 0.07432544
Outputs:
- smoothed: bfloat16 [32768, 512], P('leaf', 'parts'), parts along dimension 1
The draws below stay inside these ranges and needn't reach their ends.
There are 2 independent parts, one for each index of `parts`. The reference program is written for one: setup_inputs(seed, part) draws one part's arguments, and reference() takes and returns one part's arrays. A program takes and returns all parts, laid end to end along the dimension named above; an argument that names none is the same for every part. Nothing has to cross between parts.
All inputs are finite; a program needn't handle non-finite values.
Results may differ from the reference program's by a relative error of at most 0.0048.
Values may be sent and summed in bfloat16 or wider, within the bound.
A program may use at most 64 MiB of HBM per device.

```python
import jax
import jax.numpy as jnp
from jax import lax

LEAF = 2048
SUB = 256
NB = 3
RANK = 256
COLS = 256
SUBS = 8
LEAVES = 16
VERT = 32768
DEPTH = 4


def draw_basis(key, part):
    level = jnp.arange(DEPTH, dtype=jnp.float32)[:, None, None]
    factor = (RANK * LEAF * jnp.exp2(level)) ** (-0.25)
    limit = 2.0 * float(RANK * LEAF) ** (-0.25)
    base = jax.random.normal(key, (DEPTH, VERT, RANK), jnp.float32)
    scaled = jnp.clip(base * factor, -limit, limit)
    return scaled.astype(jnp.bfloat16)


def place_ends(drawn, key, smallest, largest):
    longest = drawn.shape.index(max(drawn.shape))
    spots = []
    for shift in (0, 1):
        where = [jax.random.randint(jax.random.fold_in(key, axis), (), 0, length) for axis, length in enumerate(drawn.shape)]
        where[longest] = (where[longest] + shift) % drawn.shape[longest]
        spots.append(tuple(where))
    return drawn.at[spots[0]].set(smallest).at[spots[1]].set(largest)


def block_scale(own_key, dims, split, low, top_value):
    loudness, own = 1.0, jax.random.fold_in(own_key, 6)
    for dim, shards_of in split:
        steps = jnp.exp(jax.random.uniform(jax.random.fold_in(own, dim), (shards_of,), jnp.float32, low / len(split), top_value / len(split)))
        loudness = loudness * jnp.repeat(steps, dims[dim] // shards_of).reshape([-1 if axis == dim else 1 for axis in range(len(dims))])
    return loudness


def scatter_about(own_key, dims, scale, bound, split=(), kind=jnp.bfloat16):
    level = block_scale(own_key, dims, split, -0.22, 0.18) if split else 1.0
    drawn = jax.random.normal(own_key, dims, jnp.float32) * scale * level
    return jnp.minimum(jnp.maximum(drawn, -bound), bound).astype(kind)


def setup_inputs(seed: int = 0, part: int = 0) -> dict:
    seeds = jax.random.split(jax.random.key(seed), 6)
    part_keys = jax.random.split(jax.random.fold_in(seeds[5], part), 6)
    features = scatter_about(part_keys[0], (VERT, COLS), 1.0, 6.0, ((0, 16),))
    vertex_order = jax.vmap(lambda own: jax.random.permutation(own, LEAF))(jax.random.split(seeds[1], LEAVES)).reshape((LEAVES, LEAF)).astype(jnp.int32)
    leaf_adjacency = place_ends(jax.random.randint(seeds[2], (LEAVES, SUBS, NB), 0, SUBS), jax.random.fold_in(seeds[2], 1), 0, SUBS - 1).astype(jnp.int32)
    near_blocks = scatter_about(seeds[3], (LEAVES, SUBS, NB, SUB, SUB), (SUB * NB) ** -0.5, 0.21875, ((0, 16),))
    basis = draw_basis(jax.random.fold_in(seeds[5], 71), part)
    return {"features": features, "vertex_order": vertex_order, "leaf_adjacency": leaf_adjacency, "near_blocks": near_blocks, "basis": basis}


def near_one(items):
    block_rows, adjacency, blocks = items
    pieces = block_rows.reshape(SUBS, SUB, COLS)
    chosen = pieces[adjacency].astype(jnp.float32)
    result = jnp.einsum("snij,snjc->sic", blocks.astype(jnp.float32), chosen)
    return result.reshape(LEAF, COLS)


def reference(features, vertex_order, leaf_adjacency, near_blocks, basis):
    blocks_in = features.reshape(LEAVES, LEAF, COLS)
    ordered = jnp.take_along_axis(blocks_in, vertex_order.astype(jnp.int32)[:, :, None], axis=1)
    total = lax.map(near_one, (ordered, leaf_adjacency, near_blocks))
    ordered_wide = ordered.astype(jnp.float32)
    for level in range(DEPTH):
        span = 2 ** level
        level_basis = basis[level].reshape(LEAVES, LEAF, RANK).astype(jnp.float32)
        projection = jnp.einsum("lvr,lvc->lrc", level_basis, ordered_wide)
        nodes = projection.reshape(LEAVES // span, span, RANK, COLS).sum(axis=1)
        pairs = nodes.reshape(LEAVES // (2 * span), 2, RANK, COLS)[:, ::-1]
        sibling = jnp.repeat(pairs.reshape(LEAVES // span, RANK, COLS), span, axis=0).astype(jnp.bfloat16)
        total = total + jnp.einsum("lvr,lrc->lvc", level_basis, sibling.astype(jnp.float32))
    return total.reshape(VERT, COLS).astype(jnp.bfloat16)
```

```python
import functools

import jax
import jax.numpy as jnp
from jax import lax
from jax.experimental import pallas as pl
from jax.experimental.pallas import tpu as pltpu
from jax.sharding import PartitionSpec as P

MESH = pl.DeviceIdType.MESH
F32 = jnp.float32
BF16 = jnp.bfloat16
MIN_CHUNK = 16
NT = (((1,), (1,)), ((), ()))


def group_bits(level, half):
    bits = level - 1
    while half >> bits < MIN_CHUNK:
        bits -= 1
    return bits


def plan(depth, half):
    ids, peers = {}, set()

    def add(key, distance):
        ids[key] = (len(ids), distance)
        peers.add(distance)

    for level in range(depth):
        if level == 0:
            add((0, "swap"), 1)
            continue
        bits = group_bits(level, half)
        add((level, "pair"), 1)
        for d in range(1, 1 << bits):
            add((level, "scatter", d), d << 1)
        for bit in range(bits + 1, level):
            add((level, "double", bit), 1 << bit)
        add((level, "swap"), 1 << level)
        for d in range(1, 1 << bits):
            add((level, "gather", d), d << 1)
        add((level, "share"), 1)
    return ids, sorted(peers)


def kernel(depth, order_ref, adj_ref, feat_hbm, near_hbm, basis_hbm, out_ref,
           feat, feat_t, ordered_t, near_v, basis_v, acc,
           proj, send, pair_in, half_out, group_in, own, chunk_out, double_in, sib,
           load_sem, send_sem, recv_sem):
    subs, nb, sub = near_v.shape[0], near_v.shape[1], near_v.shape[2]
    cols = feat.shape[1]
    half = cols // 2
    ids, peers = plan(depth, half)
    part = lax.axis_index("parts")
    me = lax.axis_index("leaf")
    core = lax.rem(me, 2)
    chip = me // 2

    def flip(index, distance):
        result = index
        bit = 0
        while distance >> bit:
            if distance >> bit & 1:
                result = result + (1 - 2 * lax.rem(index // (1 << bit), 2)) * (1 << bit)
            bit += 1
        return result

    def copy(key, src, dst):
        number, distance = ids[key]
        return pltpu.make_async_remote_copy(
            src_ref=src, dst_ref=dst, send_sem=send_sem.at[number], recv_sem=recv_sem.at[number],
            device_id=(part, flip(me, distance)), device_id_type=MESH)

    loads = [pltpu.make_async_copy(feat_hbm, feat, load_sem.at[0])]
    for level in reversed(range(depth)):
        loads.append(pltpu.make_async_copy(basis_hbm.at[level], basis_v.at[level], load_sem.at[1 + level]))
    loads.append(pltpu.make_async_copy(near_hbm.at[0], near_v, load_sem.at[1 + depth]))
    for load in loads:
        load.start()

    barrier = pltpu.get_barrier_semaphore()
    for distance in peers:
        pl.semaphore_signal(barrier, inc=1, device_id=(part, flip(me, distance)), device_id_type=MESH)

    loads[0].wait()
    for v in range(subs):
        feat_t[v] = feat[v * sub:(v + 1) * sub, :].T

    rows_in = lax.broadcasted_iota(jnp.int32, (sub, sub), 0)

    def pick(s, carry):
        wanted = order_ref[pl.ds(s, 1), :]
        total = jnp.zeros((cols, sub), F32)
        for v in range(subs):
            hot = jnp.where(rows_in == wanted - v * sub, 1.0, 0.0).astype(BF16)
            total = total + jnp.dot(feat_t[v], hot, preferred_element_type=F32)
        ordered_t[s] = total.astype(BF16)
        return carry

    lax.fori_loop(0, subs, pick, 0)

    pl.semaphore_wait(barrier, len(peers))
    started = {}

    def start(key, src, dst):
        started[key] = copy(key, src, dst)
        started[key].start()

    def mine(level):
        bits = group_bits(level, half)
        size = half >> bits
        member = lax.rem(chip, 1 << bits)
        return bits, size, member

    def far_rows(offset, size):
        return pl.ds(pl.multiple_of(offset, 16), size)

    for place, level in enumerate(reversed(range(depth))):
        loads[1 + place].wait()
        total = jnp.zeros((cols, basis_v.shape[2]), F32)
        for s in range(subs):
            total = total + jnp.dot(
                ordered_t[s], basis_v[level, s * sub:(s + 1) * sub, :], preferred_element_type=F32)
        send[level] = total.astype(BF16)
        if level == 0:
            start((0, "swap"), send.at[0], sib.at[0])
        else:
            proj[level] = total
            start((level, "pair"), send.at[level, far_rows((1 - core) * half, half)], pair_in.at[level])

    def after_pair(level):
        bits, size, member = mine(level)
        started[level, "pair"].wait_recv()
        total = proj[level, far_rows(core * half, half)] + pair_in[level].astype(F32)
        half_out[level] = total.astype(BF16)
        if bits == 0:
            return own_done(level, total, bits)
        own[level] = total
        for d in range(1, 1 << bits):
            other = flip(member, d)
            start((level, "scatter", d), half_out.at[level, far_rows(other * size, size)],
                  group_in.at[level, pl.ds((d - 1) * size, size)])

    def own_done(level, total, bits):
        size = half >> bits
        for bit in range(bits + 1, level):
            slot = bit - bits - 1
            chunk_out[level, slot, :size] = total.astype(BF16)
            start((level, "double", bit), chunk_out.at[level, slot, pl.ds(0, size)],
                  double_in.at[level, slot, pl.ds(0, size)])
            started[level, "double", bit].wait_recv()
            total = total + double_in[level, slot, :size].astype(F32)
        last = level - bits - 1
        chunk_out[level, last, :size] = total.astype(BF16)
        bits, size, member = mine(level)
        place = far_rows(core * half + member * size, size)
        start((level, "swap"), chunk_out.at[level, last, pl.ds(0, size)], sib.at[level, place])

    def after_scatter(level):
        bits, size, member = mine(level)
        if bits == 0:
            return
        total = own[level, far_rows(member * size, size)]
        for d in range(1, 1 << bits):
            started[level, "scatter", d].wait_recv()
            total = total + group_in[level, (d - 1) * size:d * size].astype(F32)
        own_done(level, total, bits)

    def after_swap(level):
        bits, size, member = mine(level)
        started[level, "swap"].wait_recv()
        place = far_rows(core * half + member * size, size)
        for d in range(1, 1 << bits):
            start((level, "gather", d), sib.at[level, place], sib.at[level, place])

    def gather_wait(level, d):
        bits, size, member = mine(level)
        place = far_rows(core * half + flip(member, d) * size, size)
        copy((level, "gather", d), sib.at[level, place], sib.at[level, place]).wait_recv()

    def after_gather(level):
        bits, size, member = mine(level)
        for d in range(1, 1 << bits):
            gather_wait(level, d)
        place = far_rows(core * half, half)
        start((level, "share"), sib.at[level, place], sib.at[level, place])

    def near_step(s, carry):
        total = jnp.zeros((sub, cols), F32)
        for k in range(nb):
            chosen = ordered_t[adj_ref[s * nb + k]]
            total = total + lax.dot_general(near_v[s, k], chosen, NT, preferred_element_type=F32)
        rows = pl.ds(pl.multiple_of(s * sub, sub), sub)
        acc[rows, :] = total
        return carry

    def far_step(levels, final):
        def body(s, carry):
            rows = pl.ds(pl.multiple_of(s * sub, sub), sub)
            total = acc[rows, :]
            for level in levels:
                total = total + lax.dot_general(
                    basis_v[level, rows, :], sib[level], NT, preferred_element_type=F32)
            if final:
                out_ref[rows, :] = total.astype(BF16)
            else:
                acc[rows, :] = total
            return carry

        lax.fori_loop(0, subs, body, 0)

    up = list(reversed(range(1, depth)))
    cut = [subs * i // 3 for i in range(4)]
    loads[1 + depth].wait()
    for level in up:
        after_pair(level)
    lax.fori_loop(cut[0], cut[1], near_step, 0)
    for level in up:
        after_scatter(level)
    lax.fori_loop(cut[1], cut[2], near_step, 0)
    for level in up:
        after_swap(level)
    lax.fori_loop(cut[2], cut[3], near_step, 0)
    for level in reversed(up):
        after_gather(level)
    started[0, "swap"].wait_recv()
    far_step([0], False)
    for level in reversed(up):
        place = far_rows((1 - core) * half, half)
        copy((level, "share"), sib.at[level, place], sib.at[level, place]).wait_recv()
    far_step(list(range(1, depth)), True)
    for key in started:
        started[key].wait_send()


def on_device(features, vertex_order, leaf_adjacency, near_blocks, basis):
    depth = lax.axis_size("leaf").bit_length() - 1
    leaf_rows, cols = features.shape
    _, subs, nb, sub, _ = near_blocks.shape
    rank = basis.shape[2]
    half = cols // 2
    count = len(plan(depth, half)[0])
    slots = max(level - group_bits(level, half) for level in range(1, depth))
    vmem = pl.BlockSpec(memory_space=pltpu.VMEM)
    hbm = pl.BlockSpec(memory_space=pl.ANY)
    return pl.pallas_call(
        functools.partial(kernel, depth),
        out_shape=jax.ShapeDtypeStruct((leaf_rows, cols), BF16),
        in_specs=[vmem, pl.BlockSpec(memory_space=pltpu.SMEM), hbm, hbm, hbm],
        out_specs=vmem,
        scratch_shapes=[
            pltpu.VMEM((leaf_rows, cols), BF16),
            pltpu.VMEM((subs, cols, sub), BF16),
            pltpu.VMEM((subs, cols, sub), BF16),
            pltpu.VMEM((subs, nb, sub, sub), BF16),
            pltpu.VMEM((depth, leaf_rows, rank), BF16),
            pltpu.VMEM((leaf_rows, cols), F32),
            pltpu.VMEM((depth, cols, rank), F32),
            pltpu.VMEM((depth, cols, rank), BF16),
            pltpu.VMEM((depth, half, rank), BF16),
            pltpu.VMEM((depth, half, rank), BF16),
            pltpu.VMEM((depth, half, rank), BF16),
            pltpu.VMEM((depth, half, rank), F32),
            pltpu.VMEM((depth, slots, half, rank), BF16),
            pltpu.VMEM((depth, slots, half, rank), BF16),
            pltpu.VMEM((depth, cols, rank), BF16),
            pltpu.SemaphoreType.DMA((2 + depth,)),
            pltpu.SemaphoreType.DMA((count,)),
            pltpu.SemaphoreType.DMA((count,)),
        ],
        compiler_params=pltpu.CompilerParams(
            collective_id=0, has_side_effects=True, vmem_limit_bytes=48 << 20),
    )(vertex_order.reshape(subs, sub), leaf_adjacency.reshape(subs * nb), features, near_blocks, basis)


def solution(mesh):
    placed = (
        P("leaf", "parts"),
        P("leaf", None),
        P("leaf", None, None),
        P("leaf", None, None, None, None),
        P(None, "leaf", None),
    )
    return jax.shard_map(
        on_device, mesh=mesh, in_specs=placed, out_specs=P("leaf", "parts"), check_vma=False
    )
```

```python
import functools

import jax
import jax.numpy as jnp
from jax import lax
from jax.experimental import pallas as pl
from jax.experimental.pallas import tpu as pltpu
from jax.sharding import PartitionSpec as P

MESH = pl.DeviceIdType.MESH
F32 = jnp.float32
BF16 = jnp.bfloat16
MIN_CHUNK = 16


def group_bits(level, half):
    bits = level - 1
    while half >> bits < MIN_CHUNK:
        bits -= 1
    return bits


def plan(depth, half):
    ids, peers = {}, set()

    def add(key, distance):
        ids[key] = (len(ids), distance)
        peers.add(distance)

    for level in range(depth):
        if level == 0:
            add((0, "swap"), 1)
            continue
        bits = group_bits(level, half)
        add((level, "pair"), 1)
        for d in range(1, 1 << bits):
            add((level, "scatter", d), d << 1)
        for bit in range(bits + 1, level):
            add((level, "double", bit), 1 << bit)
        for d in range(1 << bits):
            add((level, "swap", d), (1 << level) + (d << 1))
        add((level, "share"), 1)
    return ids, sorted(peers)


def kernel(depth, order_hbm, adj_hbm, feat_hbm, near_hbm, basis_hbm, out_ref,
           feat, feat_t, ordered_t, ordered, near_v, basis_v, acc,
           proj, send, pair_in, half_out, group_in, own, chunk_out, double_in, sib, sib_t,
           order_ref, adj_ref, load_sem, send_sem, recv_sem):
    subs, nb, sub = near_v.shape[0], near_v.shape[1], near_v.shape[2]
    cols = feat.shape[1]
    half = cols // 2
    ids, peers = plan(depth, half)
    part = lax.axis_index("parts")
    me = lax.axis_index("leaf")
    core = lax.rem(me, 2)
    chip = me // 2

    def flip(index, distance):
        result = index
        bit = 0
        while distance >> bit:
            if distance >> bit & 1:
                result = result + (1 - 2 * lax.rem(index // (1 << bit), 2)) * (1 << bit)
            bit += 1
        return result

    def copy(key, src, dst):
        number, distance = ids[key]
        return pltpu.make_async_remote_copy(
            src_ref=src, dst_ref=dst, send_sem=send_sem.at[number], recv_sem=recv_sem.at[number],
            device_id=(part, flip(me, distance)), device_id_type=MESH)

    loads = [pltpu.make_async_copy(feat_hbm, feat, load_sem.at[0])]
    for level in reversed(range(depth)):
        loads.append(pltpu.make_async_copy(basis_hbm.at[level], basis_v.at[level], load_sem.at[1 + level]))
    loads.append(pltpu.make_async_copy(near_hbm.at[0], near_v, load_sem.at[1 + depth]))
    loads.append(pltpu.make_async_copy(adj_hbm, adj_ref, load_sem.at[2 + depth]))
    order_load = pltpu.make_async_copy(order_hbm, order_ref, load_sem.at[3 + depth])
    order_load.start()
    for load in loads:
        load.start()

    barrier = pltpu.get_barrier_semaphore()
    for distance in peers:
        pl.semaphore_signal(barrier, inc=1, device_id=(part, flip(me, distance)), device_id_type=MESH)

    loads[0].wait()
    order_load.wait()
    for v in range(subs):
        feat_t[v] = feat[v * sub:(v + 1) * sub, :].T

    rows_in = lax.broadcasted_iota(jnp.int32, (sub, sub), 0)

    def pick(s, carry):
        wanted = order_ref[:, pl.ds(pl.multiple_of(s * sub, sub), sub)]
        total = jnp.zeros((cols, sub), F32)
        for v in range(subs):
            hot = jnp.where(rows_in == wanted - v * sub, 1.0, 0.0).astype(BF16)
            total = total + jnp.dot(feat_t[v], hot, preferred_element_type=F32)
        ordered_t[s] = total.astype(BF16)
        ordered[s] = total.astype(BF16).T
        return carry

    lax.fori_loop(0, subs, pick, 0, unroll=True)

    pl.semaphore_wait(barrier, len(peers))
    started = {}

    def start(key, src, dst):
        started[key] = copy(key, src, dst)
        started[key].start()

    def mine(level):
        bits = group_bits(level, half)
        size = half >> bits
        member = lax.rem(chip, 1 << bits)
        return bits, size, member

    def far_rows(offset, size):
        return pl.ds(pl.multiple_of(offset, 16), size)

    def project(level):
        loads[depth - level].wait()
        total = jnp.zeros((cols, basis_v.shape[2]), F32)
        for s in range(subs):
            total = total + jnp.dot(
                ordered_t[s], basis_v[level, s * sub:(s + 1) * sub, :], preferred_element_type=F32)
        send[level] = total.astype(BF16)
        if level == 0:
            start((0, "swap"), send.at[0], sib.at[0])
        else:
            proj[level] = total
            start((level, "pair"), send.at[level, far_rows((1 - core) * half, half)], pair_in.at[level])

    def after_pair(level):
        bits, size, member = mine(level)
        started[level, "pair"].wait_recv()
        total = proj[level, far_rows(core * half, half)] + pair_in[level].astype(F32)
        half_out[level] = total.astype(BF16)
        if bits == 0:
            return own_done(level, total, bits)
        own[level] = total
        for d in range(1, 1 << bits):
            other = flip(member, d)
            start((level, "scatter", d), half_out.at[level, far_rows(other * size, size)],
                  group_in.at[level, pl.ds((d - 1) * size, size)])

    def own_done(level, total, bits):
        size = half >> bits
        for bit in range(bits + 1, level):
            slot = bit - bits - 1
            chunk_out[level, slot, :size] = total.astype(BF16)
            start((level, "double", bit), chunk_out.at[level, slot, pl.ds(0, size)],
                  double_in.at[level, slot, pl.ds(0, size)])
            started[level, "double", bit].wait_recv()
            total = total + double_in[level, slot, :size].astype(F32)
        last = level - bits - 1
        chunk_out[level, last, :size] = total.astype(BF16)
        bits, size, member = mine(level)
        place = far_rows(core * half + member * size, size)
        for d in range(1 << bits):
            start((level, "swap", d), chunk_out.at[level, last, pl.ds(0, size)], sib.at[level, place])

    def after_scatter(level):
        bits, size, member = mine(level)
        if bits == 0:
            return
        total = own[level, far_rows(member * size, size)]
        for d in range(1, 1 << bits):
            started[level, "scatter", d].wait_recv()
            total = total + group_in[level, (d - 1) * size:d * size].astype(F32)
        own_done(level, total, bits)

    def after_swap(level):
        bits, size, member = mine(level)
        for d in range(1 << bits):
            place = far_rows(core * half + flip(member, d) * size, size)
            copy((level, "swap", d), sib.at[level, place], sib.at[level, place]).wait_recv()
        place = far_rows(core * half, half)
        start((level, "share"), sib.at[level, place], sib.at[level, place])

    def after_share(level):
        if level == 0:
            started[0, "swap"].wait_recv()
        else:
            place = far_rows((1 - core) * half, half)
            copy((level, "share"), sib.at[level, place], sib.at[level, place]).wait_recv()
        sib_t[level] = sib[level].T

    def near_step(s, carry):
        total = jnp.zeros((sub, cols), F32)
        for k in range(nb):
            chosen = ordered[adj_ref[k, 0, s]]
            total = total + jnp.dot(near_v[s, k], chosen, preferred_element_type=F32)
        rows = pl.ds(pl.multiple_of(s * sub, sub), sub)
        acc[rows, :] = total
        return carry

    tall = subs * sub

    def far_step(levels, final):
        def body(s, carry):
            rows = pl.ds(pl.multiple_of(s * tall, tall), tall)
            total = acc[rows, :]
            for level in levels:
                total = total + jnp.dot(
                    basis_v[level, rows, :], sib_t[level], preferred_element_type=F32)
            if final:
                out_ref[rows, :] = total.astype(BF16)
            else:
                acc[rows, :] = total
            return carry

        lax.fori_loop(0, subs * sub // tall, body, 0)

    up = list(reversed(range(1, depth)))
    for place, level in enumerate(reversed(range(depth))):
        project(level)
        if place >= 2:
            after_pair(up[place - 2])
    for level in up[max(depth - 2, 0):]:
        after_pair(level)
    loads[1 + depth].wait()
    loads[2 + depth].wait()
    lax.fori_loop(0, subs, near_step, 0, unroll=True)
    for level in up:
        after_scatter(level)
    after_share(0)
    far_step([0], False)
    after_swap(1)
    after_share(1)
    far_step([1], False)
    for level in reversed(up[:-1]):
        after_swap(level)
    for level in range(2, depth):
        after_share(level)
        far_step([level], level == depth - 1)
    for key in started:
        started[key].wait_send()


def on_device(features, vertex_order, leaf_adjacency, near_blocks, basis):
    depth = lax.axis_size("leaf").bit_length() - 1
    leaf_rows, cols = features.shape
    _, subs, nb, sub, _ = near_blocks.shape
    rank = basis.shape[2]
    half = cols // 2
    count = len(plan(depth, half)[0])
    slots = max(level - group_bits(level, half) for level in range(1, depth))
    vmem = pl.BlockSpec(memory_space=pltpu.VMEM)
    hbm = pl.BlockSpec(memory_space=pltpu.HBM)
    return pl.pallas_call(
        functools.partial(kernel, depth),
        out_shape=jax.ShapeDtypeStruct((leaf_rows, cols), BF16),
        in_specs=[hbm] * 5,
        out_specs=vmem,
        scratch_shapes=[
            pltpu.VMEM((leaf_rows, cols), BF16),
            pltpu.VMEM((subs, cols, sub), BF16),
            pltpu.VMEM((subs, cols, sub), BF16),
            pltpu.VMEM((subs, sub, cols), BF16),
            pltpu.VMEM((subs, nb, sub, sub), BF16),
            pltpu.VMEM((depth, leaf_rows, rank), BF16),
            pltpu.VMEM((leaf_rows, cols), F32),
            pltpu.VMEM((depth, cols, rank), F32),
            pltpu.VMEM((depth, cols, rank), BF16),
            pltpu.VMEM((depth, half, rank), BF16),
            pltpu.VMEM((depth, half, rank), BF16),
            pltpu.VMEM((depth, half, rank), BF16),
            pltpu.VMEM((depth, half, rank), F32),
            pltpu.VMEM((depth, slots, half, rank), BF16),
            pltpu.VMEM((depth, slots, half, rank), BF16),
            pltpu.VMEM((depth, cols, rank), BF16),
            pltpu.VMEM((depth, rank, cols), BF16),
            pltpu.VMEM((1, leaf_rows), jnp.int32),
            pltpu.SMEM((nb, 1, subs), jnp.int32),
            pltpu.SemaphoreType.DMA((4 + depth,)),
            pltpu.SemaphoreType.DMA((count,)),
            pltpu.SemaphoreType.DMA((count,)),
        ],
        compiler_params=pltpu.CompilerParams(
            collective_id=0, has_side_effects=True, vmem_limit_bytes=64 << 20),
    )(vertex_order, jnp.transpose(leaf_adjacency, (2, 0, 1)), features, near_blocks, basis)


def solution(mesh):
    placed = (
        P("leaf", "parts"),
        P("leaf", None),
        P("leaf", None, None),
        P("leaf", None, None, None, None),
        P(None, "leaf", None),
    )
    return jax.shard_map(
        on_device, mesh=mesh, in_specs=placed, out_specs=P("leaf", "parts"), check_vma=False
    )
```

```python
import functools

import jax
import jax.numpy as jnp
from jax import lax
from jax.experimental import pallas as pl
from jax.experimental.pallas import tpu as pltpu
from jax.sharding import PartitionSpec as P

MESH = pl.DeviceIdType.MESH
F32 = jnp.float32
BF16 = jnp.bfloat16
MIN_CHUNK = 16


def group_bits(level, half):
    bits = level - 1
    while half >> bits < MIN_CHUNK:
        bits -= 1
    return bits


def plan(depth, half):
    ids, peers = {}, set()

    def add(key, distance):
        ids[key] = (len(ids), distance)
        peers.add(distance)

    for level in range(depth):
        if level == 0:
            add((0, "swap"), 1)
            continue
        bits = group_bits(level, half)
        add((level, "pair"), 1)
        for d in range(1, 1 << bits):
            add((level, "scatter", d), d << 1)
        for bit in range(bits + 1, level):
            add((level, "double", bit), 1 << bit)
        for d in range(1 << bits):
            add((level, "swap", d), (1 << level) + (d << 1))
        add((level, "share"), 1)
    return ids, sorted(peers)


def kernel(depth, order_hbm, adj_hbm, feat_hbm, near_hbm, basis_hbm, out_ref,
           feat, feat_t, ordered_t, ordered, near_v, basis_v, acc,
           proj, send, pair_in, half_out, group_in, own, chunk_out, double_in, sib, sib_t,
           order_ref, adj_ref, load_sem, send_sem, recv_sem):
    subs, nb, sub = near_v.shape[0], near_v.shape[1], near_v.shape[2]
    cols = feat.shape[1]
    half = cols // 2
    ids, peers = plan(depth, half)
    part = lax.axis_index("parts")
    me = lax.axis_index("leaf")
    core = lax.rem(me, 2)
    chip = me // 2

    def flip(index, distance):
        result = index
        bit = 0
        while distance >> bit:
            if distance >> bit & 1:
                result = result + (1 - 2 * lax.rem(index // (1 << bit), 2)) * (1 << bit)
            bit += 1
        return result

    def copy(key, src, dst):
        number, distance = ids[key]
        return pltpu.make_async_remote_copy(
            src_ref=src, dst_ref=dst, send_sem=send_sem.at[number], recv_sem=recv_sem.at[number],
            device_id=(part, flip(me, distance)), device_id_type=MESH)

    loads = [pltpu.make_async_copy(feat_hbm, feat, load_sem.at[0])]
    for level in reversed(range(depth)):
        loads.append(pltpu.make_async_copy(basis_hbm.at[level], basis_v.at[level], load_sem.at[1 + level]))
    loads.append(pltpu.make_async_copy(near_hbm.at[0], near_v, load_sem.at[1 + depth]))
    loads.append(pltpu.make_async_copy(adj_hbm, adj_ref, load_sem.at[2 + depth]))
    order_load = pltpu.make_async_copy(order_hbm, order_ref, load_sem.at[3 + depth])
    order_load.start()
    for load in loads:
        load.start()

    barrier = pltpu.get_barrier_semaphore()
    for distance in peers:
        pl.semaphore_signal(barrier, inc=1, device_id=(part, flip(me, distance)), device_id_type=MESH)

    loads[0].wait()
    order_load.wait()
    for v in range(subs):
        feat_t[v] = feat[v * sub:(v + 1) * sub, :].T

    rows_in = lax.broadcasted_iota(jnp.int32, (sub, sub), 0)

    def pick(s, carry):
        wanted = order_ref[:, pl.ds(pl.multiple_of(s * sub, sub), sub)]
        total = jnp.zeros((cols, sub), F32)
        for v in range(subs):
            hot = jnp.where(rows_in == wanted - v * sub, 1.0, 0.0).astype(BF16)
            total = total + jnp.dot(feat_t[v], hot, preferred_element_type=F32)
        ordered_t[s] = total.astype(BF16)
        ordered[s] = total.astype(BF16).T
        return carry

    lax.fori_loop(0, subs, pick, 0, unroll=True)

    pl.semaphore_wait(barrier, len(peers))
    started = {}

    def start(key, src, dst):
        started[key] = copy(key, src, dst)
        started[key].start()

    def mine(level):
        bits = group_bits(level, half)
        size = half >> bits
        member = lax.rem(chip, 1 << bits)
        return bits, size, member

    def far_rows(offset, size):
        return pl.ds(pl.multiple_of(offset, 16), size)

    def project(level):
        loads[depth - level].wait()
        total = jnp.zeros((cols, basis_v.shape[2]), F32)
        for s in range(subs):
            total = total + jnp.dot(
                ordered_t[s], basis_v[level, s * sub:(s + 1) * sub, :], preferred_element_type=F32)
        send[level] = total.astype(BF16)
        if level == 0:
            start((0, "swap"), send.at[0], sib.at[0])
        else:
            proj[level] = total
            start((level, "pair"), send.at[level, far_rows((1 - core) * half, half)], pair_in.at[level])

    def after_pair(level):
        bits, size, member = mine(level)
        started[level, "pair"].wait_recv()
        total = proj[level, far_rows(core * half, half)] + pair_in[level].astype(F32)
        half_out[level] = total.astype(BF16)
        if bits == 0:
            return own_done(level, total, bits)
        own[level] = total
        for d in range(1, 1 << bits):
            other = flip(member, d)
            start((level, "scatter", d), half_out.at[level, far_rows(other * size, size)],
                  group_in.at[level, pl.ds((d - 1) * size, size)])

    def own_done(level, total, bits):
        size = half >> bits
        for bit in range(bits + 1, level):
            slot = bit - bits - 1
            chunk_out[level, slot, :size] = total.astype(BF16)
            start((level, "double", bit), chunk_out.at[level, slot, pl.ds(0, size)],
                  double_in.at[level, slot, pl.ds(0, size)])
            started[level, "double", bit].wait_recv()
            total = total + double_in[level, slot, :size].astype(F32)
        last = level - bits - 1
        chunk_out[level, last, :size] = total.astype(BF16)
        bits, size, member = mine(level)
        place = far_rows(core * half + member * size, size)
        for d in range(1 << bits):
            start((level, "swap", d), chunk_out.at[level, last, pl.ds(0, size)], sib.at[level, place])

    def after_scatter(level):
        bits, size, member = mine(level)
        if bits == 0:
            return
        total = own[level, far_rows(member * size, size)]
        for d in range(1, 1 << bits):
            started[level, "scatter", d].wait_recv()
            total = total + group_in[level, (d - 1) * size:d * size].astype(F32)
        own_done(level, total, bits)

    def after_swap(level):
        bits, size, member = mine(level)
        for d in range(1 << bits):
            place = far_rows(core * half + flip(member, d) * size, size)
            copy((level, "swap", d), sib.at[level, place], sib.at[level, place]).wait_recv()
        place = far_rows(core * half, half)
        start((level, "share"), sib.at[level, place], sib.at[level, place])

    def after_share(level):
        if level == 0:
            started[0, "swap"].wait_recv()
        else:
            place = far_rows((1 - core) * half, half)
            copy((level, "share"), sib.at[level, place], sib.at[level, place]).wait_recv()
        sib_t[level] = sib[level].T

    def near_step(s, carry):
        total = jnp.zeros((sub, cols), F32)
        for k in range(nb):
            chosen = ordered[adj_ref[k, 0, s]]
            total = total + jnp.dot(near_v[s, k], chosen, preferred_element_type=F32)
        rows = pl.ds(pl.multiple_of(s * sub, sub), sub)
        acc[rows, :] = total
        return carry

    tall = subs * sub

    def far_step(levels, final):
        def body(s, carry):
            rows = pl.ds(pl.multiple_of(s * tall, tall), tall)
            total = acc[rows, :]
            for level in levels:
                total = total + jnp.dot(
                    basis_v[level, rows, :], sib_t[level], preferred_element_type=F32)
            if final:
                out_ref[rows, :] = total.astype(BF16)
            else:
                acc[rows, :] = total
            return carry

        lax.fori_loop(0, subs * sub // tall, body, 0)

    up = list(reversed(range(1, depth)))
    for place, level in enumerate(reversed(range(depth))):
        project(level)
        if place >= 2:
            after_pair(up[place - 2])
    for level in up[max(depth - 2, 0):]:
        after_pair(level)
    loads[1 + depth].wait()
    loads[2 + depth].wait()
    lax.fori_loop(0, subs, near_step, 0, unroll=True)
    for level in up:
        after_scatter(level)
    after_share(0)
    far_step([0], False)
    after_swap(1)
    after_share(1)
    far_step([1], False)
    for level in reversed(up[:-1]):
        after_swap(level)
    for level in range(2, depth):
        after_share(level)
        far_step([level], level == depth - 1)
    for key in started:
        started[key].wait_send()


def on_device(features, vertex_order, leaf_adjacency, near_blocks, basis):
    depth = lax.axis_size("leaf").bit_length() - 1
    leaf_rows, cols = features.shape
    _, subs, nb, sub, _ = near_blocks.shape
    rank = basis.shape[2]
    half = cols // 2
    count = len(plan(depth, half)[0])
    slots = max(level - group_bits(level, half) for level in range(1, depth))
    vmem = pl.BlockSpec(memory_space=pltpu.VMEM)
    hbm = pl.BlockSpec(memory_space=pltpu.HBM)
    return pl.pallas_call(
        functools.partial(kernel, depth),
        out_shape=jax.ShapeDtypeStruct((leaf_rows, cols), BF16),
        in_specs=[hbm] * 5,
        out_specs=vmem,
        scratch_shapes=[
            pltpu.VMEM((leaf_rows, cols), BF16),
            pltpu.VMEM((subs, cols, sub), BF16),
            pltpu.VMEM((subs, cols, sub), BF16),
            pltpu.VMEM((subs, sub, cols), BF16),
            pltpu.VMEM((subs, nb, sub, sub), BF16),
            pltpu.VMEM((depth, leaf_rows, rank), BF16),
            pltpu.VMEM((leaf_rows, cols), F32),
            pltpu.VMEM((depth, cols, rank), F32),
            pltpu.VMEM((depth, cols, rank), BF16),
            pltpu.VMEM((depth, half, rank), BF16),
            pltpu.VMEM((depth, half, rank), BF16),
            pltpu.VMEM((depth, half, rank), BF16),
            pltpu.VMEM((depth, half, rank), F32),
            pltpu.VMEM((depth, slots, half, rank), BF16),
            pltpu.VMEM((depth, slots, half, rank), BF16),
            pltpu.VMEM((depth, cols, rank), BF16),
            pltpu.VMEM((depth, rank, cols), BF16),
            pltpu.VMEM((1, leaf_rows), jnp.int32),
            pltpu.SMEM((nb, 1, subs), jnp.int32),
            pltpu.SemaphoreType.DMA((4 + depth,)),
            pltpu.SemaphoreType.DMA((count,)),
            pltpu.SemaphoreType.DMA((count,)),
        ],
        compiler_params=pltpu.CompilerParams(
            collective_id=0, has_side_effects=True, vmem_limit_bytes=52 << 20),
    )(*[pltpu.with_memory_space_constraint(x, pltpu.HBM) for x in (vertex_order, jnp.transpose(leaf_adjacency, (2, 0, 1)), features, near_blocks, basis)])


def solution(mesh):
    placed = (
        P("leaf", "parts"),
        P("leaf", None),
        P("leaf", None, None),
        P("leaf", None, None, None, None),
        P(None, "leaf", None),
    )
    return jax.shard_map(
        on_device, mesh=mesh, in_specs=placed, out_specs=P("leaf", "parts"), check_vma=False
    )
```

```python
import functools

import jax
import jax.numpy as jnp
from jax import lax
from jax.experimental import pallas as pl
from jax.experimental.pallas import tpu as pltpu
from jax.sharding import PartitionSpec as P

MESH = pl.DeviceIdType.MESH
F32 = jnp.float32
BF16 = jnp.bfloat16
MIN_CHUNK = 16


def group_bits(level, half):
    bits = level - 1
    while half >> bits < MIN_CHUNK:
        bits -= 1
    return bits


def plan(depth, half):
    ids, peers = {}, set()

    def add(key, distance):
        ids[key] = (len(ids), distance)
        peers.add(distance)

    for level in range(depth):
        if level == 0:
            add((0, "swap"), 1)
            continue
        bits = group_bits(level, half)
        add((level, "pair"), 1)
        for d in range(1, 1 << bits):
            add((level, "scatter", d), d << 1)
        for bit in range(bits + 1, level):
            add((level, "double", bit), 1 << bit)
        for d in range(1 << bits):
            add((level, "swap", d), (1 << level) + (d << 1))
        add((level, "share"), 1)
    return ids, sorted(peers)


def kernel(depth, order_hbm, adj_hbm, feat_hbm, near_hbm, basis_hbm, out_ref,
           feat, feat_t, ordered_t, ordered, near_v, basis_v, acc,
           proj, send, pair_in, half_out, group_in, own, chunk_out, double_in, sib, sib_t,
           order_ref, adj_ref, load_sem, send_sem, recv_sem):
    subs, nb, sub = near_v.shape[0], near_v.shape[1], near_v.shape[2]
    cols = feat.shape[1]
    half = cols // 2
    ids, peers = plan(depth, half)
    part = lax.axis_index("parts")
    me = lax.axis_index("leaf")
    core = lax.rem(me, 2)
    chip = me // 2

    def flip(index, distance):
        result = index
        bit = 0
        while distance >> bit:
            if distance >> bit & 1:
                result = result + (1 - 2 * lax.rem(index // (1 << bit), 2)) * (1 << bit)
            bit += 1
        return result

    def copy(key, src, dst):
        number, distance = ids[key]
        return pltpu.make_async_remote_copy(
            src_ref=src, dst_ref=dst, send_sem=send_sem.at[number], recv_sem=recv_sem.at[number],
            device_id=(part, flip(me, distance)), device_id_type=MESH)

    loads = [pltpu.make_async_copy(feat_hbm, feat, load_sem.at[0])]
    for level in reversed(range(depth)):
        loads.append(pltpu.make_async_copy(basis_hbm.at[level], basis_v.at[level], load_sem.at[1 + level]))
    loads.append(pltpu.make_async_copy(near_hbm.at[0], near_v, load_sem.at[1 + depth]))
    loads.append(pltpu.make_async_copy(adj_hbm, adj_ref, load_sem.at[2 + depth]))
    order_load = pltpu.make_async_copy(order_hbm, order_ref, load_sem.at[3 + depth])
    order_load.start()
    loads[0].start()

    barrier = pltpu.get_barrier_semaphore()
    for distance in peers:
        pl.semaphore_signal(barrier, inc=1, device_id=(part, flip(me, distance)), device_id_type=MESH)

    loads[0].wait()
    order_load.wait()
    for load in loads[1:]:
        load.start()
    for v in range(subs):
        feat_t[v] = feat[v * sub:(v + 1) * sub, :].T

    rows_in = lax.broadcasted_iota(jnp.int32, (sub, sub), 0)

    def pick(s, carry):
        wanted = order_ref[:, pl.ds(pl.multiple_of(s * sub, sub), sub)]
        total = jnp.zeros((cols, sub), F32)
        for v in range(subs):
            hot = jnp.where(rows_in == wanted - v * sub, 1.0, 0.0).astype(BF16)
            total = total + jnp.dot(feat_t[v], hot, preferred_element_type=F32)
        ordered_t[s] = total.astype(BF16)
        return carry

    lax.fori_loop(0, subs, pick, 0, unroll=True)

    pl.semaphore_wait(barrier, len(peers))
    started = {}

    def start(key, src, dst):
        started[key] = copy(key, src, dst)
        started[key].start()

    def mine(level):
        bits = group_bits(level, half)
        size = half >> bits
        member = lax.rem(chip, 1 << bits)
        return bits, size, member

    def far_rows(offset, size):
        return pl.ds(pl.multiple_of(offset, 16), size)

    def project(level):
        loads[depth - level].wait()
        total = jnp.zeros((cols, basis_v.shape[2]), F32)
        for s in range(subs):
            total = total + jnp.dot(
                ordered_t[s], basis_v[level, s * sub:(s + 1) * sub, :], preferred_element_type=F32)
        send[level] = total.astype(BF16)
        if level == 0:
            start((0, "swap"), send.at[0], sib.at[0])
        else:
            proj[level] = total
            start((level, "pair"), send.at[level, far_rows((1 - core) * half, half)], pair_in.at[level])

    def after_pair(level):
        bits, size, member = mine(level)
        started[level, "pair"].wait_recv()
        total = proj[level, far_rows(core * half, half)] + pair_in[level].astype(F32)
        half_out[level] = total.astype(BF16)
        if bits == 0:
            return own_done(level, total, bits)
        own[level] = total
        for d in range(1, 1 << bits):
            other = flip(member, d)
            start((level, "scatter", d), half_out.at[level, far_rows(other * size, size)],
                  group_in.at[level, pl.ds((d - 1) * size, size)])

    def own_done(level, total, bits):
        size = half >> bits
        for bit in range(bits + 1, level):
            slot = bit - bits - 1
            chunk_out[level, slot, :size] = total.astype(BF16)
            start((level, "double", bit), chunk_out.at[level, slot, pl.ds(0, size)],
                  double_in.at[level, slot, pl.ds(0, size)])
            started[level, "double", bit].wait_recv()
            total = total + double_in[level, slot, :size].astype(F32)
        last = level - bits - 1
        chunk_out[level, last, :size] = total.astype(BF16)
        bits, size, member = mine(level)
        place = far_rows(core * half + member * size, size)
        for d in range(1 << bits):
            start((level, "swap", d), chunk_out.at[level, last, pl.ds(0, size)], sib.at[level, place])

    def after_scatter(level):
        bits, size, member = mine(level)
        if bits == 0:
            return
        total = own[level, far_rows(member * size, size)]
        for d in range(1, 1 << bits):
            started[level, "scatter", d].wait_recv()
            total = total + group_in[level, (d - 1) * size:d * size].astype(F32)
        own_done(level, total, bits)

    def after_swap(level):
        bits, size, member = mine(level)
        for d in range(1 << bits):
            place = far_rows(core * half + flip(member, d) * size, size)
            copy((level, "swap", d), sib.at[level, place], sib.at[level, place]).wait_recv()
        place = far_rows(core * half, half)
        start((level, "share"), sib.at[level, place], sib.at[level, place])

    def after_share(level):
        if level == 0:
            started[0, "swap"].wait_recv()
        else:
            place = far_rows((1 - core) * half, half)
            copy((level, "share"), sib.at[level, place], sib.at[level, place]).wait_recv()
        sib_t[level] = sib[level].T

    def near_step(s, carry):
        total = jnp.zeros((sub, cols), F32)
        for k in range(nb):
            chosen = ordered[adj_ref[k, 0, s]]
            total = total + jnp.dot(near_v[s, k], chosen, preferred_element_type=F32)
        rows = pl.ds(pl.multiple_of(s * sub, sub), sub)
        acc[rows, :] = total
        return carry

    tall = subs * sub

    def far_step(levels, final):
        def body(s, carry):
            rows = pl.ds(pl.multiple_of(s * tall, tall), tall)
            total = acc[rows, :]
            for level in levels:
                total = total + jnp.dot(
                    basis_v[level, rows, :], sib_t[level], preferred_element_type=F32)
            if final:
                out_ref[rows, :] = total.astype(BF16)
            else:
                acc[rows, :] = total
            return carry

        lax.fori_loop(0, subs * sub // tall, body, 0)

    up = list(reversed(range(1, depth)))
    for place, level in enumerate(reversed(range(depth))):
        project(level)
        if place >= 2:
            after_pair(up[place - 2])
    for level in up[max(depth - 2, 0):]:
        after_pair(level)
    loads[1 + depth].wait()
    loads[2 + depth].wait()
    for s in range(subs):
        ordered[s] = ordered_t[s].T
    lax.fori_loop(0, subs, near_step, 0, unroll=True)
    for level in up:
        after_scatter(level)
    after_share(0)
    far_step([0], False)
    after_swap(1)
    after_share(1)
    far_step([1], False)
    for level in reversed(up[:-1]):
        after_swap(level)
    for level in range(2, depth):
        after_share(level)
        far_step([level], level == depth - 1)
    for key in started:
        started[key].wait_send()


def on_device(features, vertex_order, leaf_adjacency, near_blocks, basis):
    depth = lax.axis_size("leaf").bit_length() - 1
    leaf_rows, cols = features.shape
    _, subs, nb, sub, _ = near_blocks.shape
    rank = basis.shape[2]
    half = cols // 2
    count = len(plan(depth, half)[0])
    slots = max(level - group_bits(level, half) for level in range(1, depth))
    vmem = pl.BlockSpec(memory_space=pltpu.VMEM)
    hbm = pl.BlockSpec(memory_space=pltpu.HBM)
    return pl.pallas_call(
        functools.partial(kernel, depth),
        out_shape=jax.ShapeDtypeStruct((leaf_rows, cols), BF16),
        in_specs=[hbm] * 5,
        out_specs=vmem,
        scratch_shapes=[
            pltpu.VMEM((leaf_rows, cols), BF16),
            pltpu.VMEM((subs, cols, sub), BF16),
            pltpu.VMEM((subs, cols, sub), BF16),
            pltpu.VMEM((subs, sub, cols), BF16),
            pltpu.VMEM((subs, nb, sub, sub), BF16),
            pltpu.VMEM((depth, leaf_rows, rank), BF16),
            pltpu.VMEM((leaf_rows, cols), F32),
            pltpu.VMEM((depth, cols, rank), F32),
            pltpu.VMEM((depth, cols, rank), BF16),
            pltpu.VMEM((depth, half, rank), BF16),
            pltpu.VMEM((depth, half, rank), BF16),
            pltpu.VMEM((depth, half, rank), BF16),
            pltpu.VMEM((depth, half, rank), F32),
            pltpu.VMEM((depth, slots, half, rank), BF16),
            pltpu.VMEM((depth, slots, half, rank), BF16),
            pltpu.VMEM((depth, cols, rank), BF16),
            pltpu.VMEM((depth, rank, cols), BF16),
            pltpu.VMEM((1, leaf_rows), jnp.int32),
            pltpu.SMEM((nb, 1, subs), jnp.int32),
            pltpu.SemaphoreType.DMA((4 + depth,)),
            pltpu.SemaphoreType.DMA((count,)),
            pltpu.SemaphoreType.DMA((count,)),
        ],
        compiler_params=pltpu.CompilerParams(
            collective_id=0, has_side_effects=True, vmem_limit_bytes=52 << 20),
    )(*[pltpu.with_memory_space_constraint(x, pltpu.HBM) for x in (vertex_order, jnp.transpose(leaf_adjacency, (2, 0, 1)), features, near_blocks, basis)])


def solution(mesh):
    placed = (
        P("leaf", "parts"),
        P("leaf", None),
        P("leaf", None, None),
        P("leaf", None, None, None, None),
        P(None, "leaf", None),
    )
    return jax.shard_map(
        on_device, mesh=mesh, in_specs=placed, out_specs=P("leaf", "parts"), check_vma=False
    )
```
